32 devices in a mesh: gx: 8 (over z, x), gy: 2 (over y), gz: 2 (over core).
Axes of the slice: x: 2, y: 2, z: 4, core: 2. Of those that a mesh axis runs over, the one named last changes fastest.
Arguments:
- velocity: float32 [3, 128, 64, 256], P(None, 'gx', 'gy', 'gz'), may hold values from -6 to 6
- conv_prev: float32 [3, 128, 64, 256], P(None, 'gx', 'gy', 'gz'), may hold values from -8 to 8
Outputs:
- convection: float32 [3, 128, 64, 256], P(None, 'gx', 'gy', 'gz')
- updated: float32 [3, 128, 64, 256], P(None, 'gx', 'gy', 'gz')
The draws below stay inside these ranges and needn't reach their ends.
All inputs are finite; a program needn't handle non-finite values.
Results may differ from the reference program's by a relative error of at most 0.00011.
Values sent between devices are 32-bit elements; how exact they have to be, the bound alone decides.
A program may use at most 64 MiB of HBM per device.

```python
import jax
import jax.numpy as jnp
from jax import lax

CY = 32
NX = 128
NY = 64
NZ = 256


def draw_velocity(key, part):
    noise_key, factor_key = jax.random.split(key)
    shape = (3, NX, NY, NZ)
    factor = jnp.exp(jax.random.uniform(factor_key, shape, jnp.float32, -0.5, 0.5))
    values = jax.random.truncated_normal(noise_key, -4.0, 4.0, shape, jnp.float32) * factor
    return jnp.clip(values, -6.0, 6.0)


def block_scale(rng, shape, cuts, least, largest):
    level, own = 1.0, jax.random.fold_in(rng, 6)
    for position, shards_of in cuts:
        heights = jnp.exp(jax.random.uniform(jax.random.fold_in(own, position), (shards_of,), jnp.float32, least / len(cuts), largest / len(cuts)))
        level = level * jnp.repeat(heights, shape[position] // shards_of).reshape([-1 if axis == position else 1 for axis in range(len(shape))])
    return level


def bell_draw(stream_key, extent, scale, most, shards=(), held_as=jnp.bfloat16):
    array = scale * jax.random.normal(stream_key, extent, jnp.float32)
    if shards:
        array = array * block_scale(stream_key, extent, shards, -0.22, 0.18)
    return jnp.clip(array, -most, most).astype(held_as)


def setup_inputs(seed: int = 0) -> dict:
    key_list = jax.random.split(jax.random.key(seed), 3)
    return {
        "velocity": draw_velocity(jax.random.fold_in(key_list[2], 71), 0),
        "conv_prev": bell_draw(key_list[1], (3, NX, NY, NZ), 2.0, 8.0, ((1, 8), (2, 2), (3, 2)), jnp.float32),
    }


time_step = 1.0
gamma_now = 5.0 / 12.0
zeta_old = -17.0 / 60.0
viscosity = 0.1


def line_table(off_value, center, total):
    def advance(previous, unused):
        pivot = center - off_value * previous
        ratio = off_value / pivot
        return ratio, (ratio, pivot)

    _, (ratios, pivots) = lax.scan(advance, jnp.zeros((), jnp.float32), None, length=total)
    return ratios, pivots


def thomas(values, off_value, center, axis):
    moved = jnp.moveaxis(values, axis, 0)
    ratios, pivots = line_table(off_value, center, moved.shape[0])

    def forward(carry, items):
        value, ratio, pivot = items
        fresh = value / pivot - ratio * carry
        return fresh, fresh

    _, reduced = lax.scan(forward, jnp.zeros(moved.shape[1:], jnp.float32), (moved, ratios, pivots))

    def backward(carry, items):
        value, ratio = items
        fresh = value - ratio * carry
        return fresh, fresh

    _, solved = lax.scan(backward, jnp.zeros(moved.shape[1:], jnp.float32), (reduced, ratios), reverse=True)
    return jnp.moveaxis(solved, 0, axis)


def compact_sides(field, axis):
    total = field.shape[axis]
    widths = [(0, 0), (0, 0), (0, 0)]
    widths[axis] = (2, 2)
    padded = jnp.pad(field, widths)

    def shifted(shift):
        return lax.slice_in_dim(padded, 2 + shift, 2 + shift + total, axis=axis)

    centre = shifted(0)
    first = (7.0 / 9.0) * (shifted(1) - shifted(-1)) + (1.0 / 36.0) * (shifted(2) - shifted(-2))
    second = (12.0 / 11.0) * (shifted(1) - 2.0 * centre + shifted(-1)) + (3.0 / 44.0) * (shifted(2) - 2.0 * centre + shifted(-2))
    return first, second


def span_terms(field):
    def shifted(shift):
        return jnp.roll(field, -shift, axis=2)

    first = (45.0 * (shifted(1) - shifted(-1)) - 9.0 * (shifted(2) - shifted(-2)) + (shifted(3) - shifted(-3))) / 60.0
    second = (2.0 * (shifted(3) + shifted(-3)) - 27.0 * (shifted(2) + shifted(-2)) + 270.0 * (shifted(1) + shifted(-1)) - 490.0 * field) / 180.0
    return first, second


def reference(velocity, conv_prev):
    beta = 4.0 * CY * CY

    def component(index):
        field = velocity[index]
        rhs_first, rhs_second = compact_sides(field, 0)
        first_x = thomas(rhs_first, 1.0 / 3.0, 1.0, 0)
        second_x = thomas(rhs_second, 2.0 / 11.0, 1.0, 0)
        rhs_first, rhs_second = compact_sides(field, 1)
        first_y = thomas(rhs_first, 1.0 / 3.0, 1.0, 1)
        second_y = thomas(rhs_second, 2.0 / 11.0, 1.0, 1)
        first_z, second_z = span_terms(field)
        convection = velocity[0] * first_x + velocity[1] * first_y + velocity[2] * first_z
        explicit = field - time_step * (gamma_now * convection + zeta_old * conv_prev[index]) + viscosity * (second_x + second_y + second_z)
        updated = thomas(explicit, -beta, 1.0 + 2.0 * beta, 1)
        return convection, updated

    convection, updated = lax.map(component, jnp.arange(3))
    return convection, updated
```

```python
import collections
import functools

import jax
import jax.numpy as jnp
import numpy as np
from jax import lax
from jax.experimental import pallas as pl
from jax.experimental.pallas import tpu as pltpu
from jax.sharding import PartitionSpec as P

MESH = pl.DeviceIdType.MESH
time_step = 1.0
gamma_now = 5.0 / 12.0
zeta_old = -17.0 / 60.0
viscosity = 0.1

FIRST = {1: 7.0 / 9.0, -1: -7.0 / 9.0, 2: 1.0 / 36.0, -2: -1.0 / 36.0}
SECOND = {1: 12.0 / 11.0, -1: 12.0 / 11.0, 2: 3.0 / 44.0, -2: 3.0 / 44.0, 0: -24.0 / 11.0 - 6.0 / 44.0}
COMPACT = ((1.0 / 3.0, 1.0, FIRST), (2.0 / 11.0, 1.0, SECOND))


class System:
    def __init__(self, off, mid, stencil, count, m):
        n = count * m
        rho = np.zeros(n + 2)
        last = 0.0
        for j in range(n + 2):
            last = -off / (mid + off * last)
            rho[j] = last

        def u(j, ref):
            if j < 0:
                return 0.0
            if j <= ref:
                return float(np.prod(rho[j:ref]))
            return 1.0 / float(np.prod(rho[ref:j]))

        def v(j, ref):
            return u(n - 1 - j, n - 1 - ref)

        def inv(i, j):
            low = rho[i - 1] if i > 0 else 0.0
            high = rho[n - 2 - i] if i < n - 1 else 0.0
            diag = 1.0 / (mid + off * low + off * high)
            return diag * (u(j, i) if j <= i else v(j, i))

        def b(j, col):
            return stencil.get(col - j, 0.0)

        self.off, self.m, self.count = off, m, count
        self.right, self.left = np.zeros((count, m)), np.zeros((count, m))
        self.fix_low, self.fix_high = np.zeros((count, 3)), np.zeros((count, 3))
        self.d = np.zeros((count, 4))
        self.t = np.zeros((count, 2))
        self.weights = np.zeros((2, count, 2, count))
        for p in range(count):
            start, end = p * m, p * m + m - 1
            for k in range(m):
                col = start + k
                rows = [j for j in range(col - 2, col + 3) if 0 <= j < n]
                self.right[p, k] = sum(u(j, end) * b(j, col) for j in rows)
                self.left[p, k] = sum(v(j, start) * b(j, col) for j in rows)
            if p > 0:
                e = start - 1
                self.fix_low[p] = (
                    sum((inv(e, j) - inv(e, e) * u(j, e)) * b(j, e) for j in (e + 1, e + 2)),
                    (inv(e, e + 1) - inv(e, e) * u(e + 1, e)) * b(e + 1, e - 1),
                    (inv(e, e - 1) - inv(e, e + 1) * v(e - 1, e + 1)) * b(e - 1, e + 1),
                )
                self.d[p, 0], self.d[p, 1] = inv(e, e), inv(e, e + 1)
                self.t[p, 0] = u(e, end)
                for q in range(count):
                    if q < p:
                        self.weights[0, q, 0, p] = inv(e, q * m + m - 1)
                    else:
                        self.weights[0, q, 1, p] = inv(e, q * m)
            if p < count - 1:
                f = end + 1
                self.fix_high[p] = (
                    sum((inv(f, j) - inv(f, f) * v(j, f)) * b(j, f) for j in (f - 1, f - 2)),
                    (inv(f, f - 1) - inv(f, f) * v(f - 1, f)) * b(f - 1, f + 1),
                    (inv(f, f + 1) - inv(f, f - 1) * u(f + 1, f - 1)) * b(f + 1, f - 1),
                )
                self.d[p, 2], self.d[p, 3] = inv(f, f - 1), inv(f, f)
                self.t[p, 1] = v(f, start)
                for q in range(count):
                    if q > p:
                        self.weights[1, q, 1, p] = inv(f, q * m)
                    else:
                        self.weights[1, q, 0, p] = inv(f, q * m + m - 1)
        pivots, ratios, last = [], [], 0.0
        for _ in range(m):
            pivot = mid - off * last
            last = off / pivot
            pivots.append(pivot)
            ratios.append(last)
        self.scale = [float(1.0 / pivot) for pivot in pivots]
        self.ratio = [float(ratio) for ratio in ratios]
        unit = np.zeros(m)
        unit[0] = 1.0
        self.low = [-off * value for value in self.solve(list(unit))]
        self.high = self.low[::-1]

    def solve(self, rows):
        done, carry = [], None
        for i, row in enumerate(rows):
            fresh = row * self.scale[i]
            carry = fresh if carry is None else fresh - self.ratio[i] * carry
            done.append(carry)
        for i in range(self.m - 2, -1, -1):
            done[i] = done[i] - self.ratio[i] * done[i + 1]
        return done


def pick(place, values):
    values = [float(np.float32(value)) for value in values]
    common = collections.Counter(values).most_common(1)[0][0]
    result = jnp.float32(common)
    for index, value in enumerate(values):
        if value != common:
            result = jnp.where(place == index, jnp.float32(value), result)
    return result


def sides(at):
    odd_1, even_1 = at(1) - at(-1), at(1) + at(-1)
    odd_2, even_2 = at(2) - at(-2), at(2) + at(-2)
    first = FIRST[1] * odd_1 + FIRST[2] * odd_2
    second = SECOND[1] * even_1 + (SECOND[2] * even_2 + SECOND[0] * at(0))
    return first, second


def total(terms):
    return functools.reduce(lambda a, b: a + b, terms)


def kernel(
    cfg, v, cp, conv, upd,
    zo, xlo, xhi, ypack, ylo, yhi, gx, gr, to, ti, gy, gyr, gw, gwr,
    fx, sx, fy, sy, expl,
    t1s, t1r, t2s, t2r, xs, xr, ys, yr, gys, gyrs, ws, wr, zs, zr,
):
    nc, mx, my, nz, px, py, units = cfg
    real = len(COMPACT) * nc * (my // 8)
    me = lax.axis_index("gx")
    wall = lax.axis_index("gy")
    core = lax.axis_index("gz")
    sys_x = [System(*pair, px, mx) for pair in COMPACT]
    sys_y = [System(*pair, py, my) for pair in COMPACT]
    beta = 4.0 * my * my
    sys_w = System(-beta, 1.0 + 2.0 * beta, {0: 1.0}, py, my)

    def gx_peer(d):
        return lax.rem(me + d, px)

    def gy_peer(d):
        return lax.rem(wall + d, py)

    barrier = pltpu.get_barrier_semaphore()
    for d in range(1, px):
        pl.semaphore_signal(barrier, inc=1, device_id={"gx": gx_peer(d)}, device_id_type=MESH)
    for d in range(1, py):
        pl.semaphore_signal(barrier, inc=1, device_id={"gy": gy_peer(d)}, device_id_type=MESH)
    pl.semaphore_signal(barrier, inc=1, device_id={"gz": 1 - core}, device_id_type=MESH)

    def remote(src, dst, send, recv, **target):
        return pltpu.make_async_remote_copy(
            src_ref=src, dst_ref=dst, send_sem=send, recv_sem=recv,
            device_id=target, device_id_type=MESH,
        )

    per = nc * (my // 8)
    for s in range(2):
        right = [pick(me, sys_x[s].right[:, i]) for i in range(mx)]
        left = [pick(me, sys_x[s].left[:, i]) for i in range(mx)]

        def sums_x(c, _, s=s, right=right, left=left):
            rows = [v[c, pl.ds(i * my, my), :] for i in range(mx)]
            for way, table in ((0, right), (1, left)):
                value = total([table[i] * rows[i] for i in range(mx)])
                gx[way, pl.ds(s * per + c * (my // 8), my // 8)] = value.reshape(my // 8, 8, nz)
            return 0

        lax.fori_loop(0, nc, sums_x, 0)
    if px * units > real:
        gx[:, pl.ds(real, px * units - real)] = jnp.zeros((2, px * units - real, 8, nz), jnp.float32)

    pl.semaphore_wait(barrier, px - 1 + py - 1 + 1)

    first_round = []
    for d in range(1, px):
        t = gx_peer(d)
        source = gx_peer(px - d)
        copy = remote(
            gx.at[:, pl.ds(t * units, units)], gr.at[me], t1s.at[d], t1r.at[d], gx=t
        )
        copy.start()
        first_round.append((copy, source))
    gr[me] = gx[:, pl.ds(me * units, units)]

    up = remote(v.at[:, pl.ds((mx - 2) * my, 2 * my)], xlo, xs.at[0], xr.at[0], gx=gx_peer(1))
    down = remote(v.at[:, pl.ds(0, 2 * my)], xhi, xs.at[1], xr.at[1], gx=gx_peer(px - 1))

    @pl.when(me < px - 1)
    def _():
        up.start()

    @pl.when(me > 0)
    def _():
        down.start()

    z_copies = []
    for c in range(nc):
        copy = remote(v.at[c], zo.at[c], zs.at[c], zr.at[c], gz=1 - core)
        copy.start()
        z_copies.append(copy)

    def yrow(ref, c, y):
        return ref[c, pl.ds(y, mx, stride=my), :]

    for c in range(nc):
        for side, first in ((0, my - 2), (1, 0)):
            for k in range(2):
                ypack[side, k, c] = yrow(v, c, first + k)
    y_up = remote(ypack.at[0], ylo, ys.at[0], yr.at[0], gy=gy_peer(1))
    y_down = remote(ypack.at[1], yhi, ys.at[1], yr.at[1], gy=gy_peer(py - 1))

    @pl.when(wall < py - 1)
    def _():
        y_up.start()

    @pl.when(wall > 0)
    def _():
        y_down.start()

    for s in range(2):
        right = [pick(wall, sys_y[s].right[:, i]) for i in range(my)]
        left = [pick(wall, sys_y[s].left[:, i]) for i in range(my)]

        def sums_y(c, _, s=s, right=right, left=left):
            low = high = None
            for i in range(my):
                row = yrow(v, c, i)
                low = right[i] * row if low is None else low + right[i] * row
                high = left[i] * row if high is None else high + left[i] * row
            gy[0, s, c] = low
            gy[1, s, c] = high
            return 0

        lax.fori_loop(0, nc, sums_y, 0)
    gy_copies = []
    for d in range(1, py):
        copy = remote(gy, gyr.at[wall], gys.at[d], gyrs.at[d], gy=gy_peer(d))
        copy.start()
        gy_copies.append(copy)
    gyr[wall] = gy[...]

    @pl.when(me > 0)
    def _():
        up.wait_recv()

    @pl.when(me == 0)
    def _():
        xlo[...] = jnp.zeros_like(xlo)

    @pl.when(me < px - 1)
    def _():
        down.wait_recv()

    @pl.when(me == px - 1)
    def _():
        xhi[...] = jnp.zeros_like(xhi)

    low_x = [[pick(me, -s.off * s.fix_low[:, k]) for k in range(3)] for s in sys_x]
    high_x = [[pick(me, -s.off * s.fix_high[:, k]) for k in range(3)] for s in sys_x]
    tile = 16 if my % 16 == 0 else 8

    def solve_x(index, _):
        c = index // (my // tile)
        base = lax.rem(index, my // tile) * tile
        rows = [xlo[c, pl.ds(k * my + base, tile), :] for k in range(2)]
        rows += [v[c, pl.ds(i * my + base, tile), :] for i in range(mx)]
        rows += [xhi[c, pl.ds(k * my + base, tile), :] for k in range(2)]
        pairs = [sides(lambda k, i=i: rows[i + 2 + k]) for i in range(mx)]
        for s, out in ((0, fx), (1, sx)):
            rhs = [pair[s] for pair in pairs]
            rhs[0] = rhs[0] + (
                low_x[s][0] * rows[1] + low_x[s][1] * rows[0] + low_x[s][2] * rows[2]
            )
            rhs[mx - 1] = rhs[mx - 1] + (
                high_x[s][0] * rows[mx + 2] + high_x[s][1] * rows[mx + 3] + high_x[s][2] * rows[mx + 1]
            )
            for i, value in enumerate(sys_x[s].solve(rhs)):
                out[c, pl.ds(i * my + base, tile), :] = value
        return 0

    lax.fori_loop(0, nc * (my // tile), solve_x, 0)

    for copy, _ in first_round:
        copy.wait_recv()
    share = jnp.minimum(me * units // per, 1)

    def both(field):
        return [pick(share, [field(sys_x[0], p), field(sys_x[1], p)]) for p in range(px)]

    t0, t1 = (both(lambda s, p, k=k: s.t[p, k]) for k in range(2))
    d0, d1, d2, d3 = (both(lambda s, p, k=k: s.d[p, k]) for k in range(4))
    below, above = [None] * px, [None] * px
    for p in range(px):
        here = gr[p, 0]
        below[p] = here if p == 0 else here + t0[p] * below[p - 1]
    for p in reversed(range(px)):
        here = gr[p, 1]
        above[p] = here if p == px - 1 else here + t1[p] * above[p + 1]
    for p in range(px):
        zero = jnp.zeros((units, 8, nz), jnp.float32)
        to[p, 0] = zero if p == 0 else d0[p] * below[p - 1] + d1[p] * above[p]
        to[p, 1] = zero if p == px - 1 else d2[p] * below[p] + d3[p] * above[p + 1]
    second_round = []
    for d in range(1, px):
        t = gx_peer(d)
        copy = remote(to.at[t], ti.at[:, pl.ds(me * units, units)], t2s.at[d], t2r.at[d], gx=t)
        copy.start()
        second_round.append(copy)
    ti[:, pl.ds(me * units, units)] = to[me]

    @pl.when(wall > 0)
    def _():
        y_up.wait_recv()

    @pl.when(wall == 0)
    def _():
        ylo[...] = jnp.zeros_like(ylo)

    @pl.when(wall < py - 1)
    def _():
        y_down.wait_recv()

    @pl.when(wall == py - 1)
    def _():
        yhi[...] = jnp.zeros_like(yhi)

    for copy in gy_copies:
        copy.wait_recv()

    def gathered(system, side):
        return [[pick(wall, system.weights[side, q, way]) for way in range(2)] for q in range(py)]

    low_y = [[pick(wall, -s.off * s.fix_low[:, k]) for k in range(3)] for s in sys_y]
    high_y = [[pick(wall, -s.off * s.fix_high[:, k]) for k in range(3)] for s in sys_y]
    outer_y = [[gathered(s, side) for side in range(2)] for s in sys_y]

    def solve_y(index, _):
        c = index // (mx // 8)
        base = lax.rem(index, mx // 8) * 8
        part = pl.ds(base, 8)
        rows = [ylo[k, c, part, :] for k in range(2)]
        rows += [v[c, pl.ds(base * my + y, 8, stride=my), :] for y in range(my)]
        rows += [yhi[k, c, part, :] for k in range(2)]
        pairs = [sides(lambda k, i=i: rows[i + 2 + k]) for i in range(my)]
        for s, out in ((0, fy), (1, sy)):
            rhs = [pair[s] for pair in pairs]
            ends = [
                total([
                    outer_y[s][side][q][way] * gyr[q, way, s, c, part, :]
                    for q in range(py) for way in range(2)
                ])
                for side in range(2)
            ]
            rhs[0] = rhs[0] + (
                low_y[s][0] * rows[1] + low_y[s][1] * rows[0] + low_y[s][2] * rows[2]
                - sys_y[s].off * ends[0]
            )
            rhs[my - 1] = rhs[my - 1] + (
                high_y[s][0] * rows[my + 2] + high_y[s][1] * rows[my + 3] + high_y[s][2] * rows[my + 1]
                - sys_y[s].off * ends[1]
            )
            for i, value in enumerate(sys_y[s].solve(rhs)):
                out[c, pl.ds(base * my + i, 8, stride=my), :] = value
        return 0

    lax.fori_loop(0, nc * (mx // 8), solve_y, 0)

    for copy in z_copies:
        copy.wait_recv()

    def solve_z(index, _):
        c = index // mx
        part = pl.ds(lax.rem(index, mx) * my, my)
        own, other = v[c, part, :], zo[c, part, :]
        lane = lax.broadcasted_iota(jnp.int32, own.shape, 1)

        def ahead(k):
            return pltpu.roll(jnp.where(lane < k, other, own), nz - k, 1)

        def back(k):
            return pltpu.roll(jnp.where(lane >= nz - k, other, own), k, 1)

        p1, m1, p2, m2, p3, m3 = ahead(1), back(1), ahead(2), back(2), ahead(3), back(3)
        first = (45.0 / 60.0) * (p1 - m1) - (9.0 / 60.0) * (p2 - m2) + (1.0 / 60.0) * (p3 - m3)
        second = (
            (2.0 / 180.0) * (p3 + m3) - (27.0 / 180.0) * (p2 + m2)
            + (270.0 / 180.0) * (p1 + m1) - (490.0 / 180.0) * own
        )
        moved = v[0, part, :] * fx[c, part, :] + v[1, part, :] * fy[c, part, :] + v[2, part, :] * first
        conv[c, part, :] = moved
        expl[c, part, :] = (
            own - time_step * (gamma_now * moved + zeta_old * cp[c, part, :])
            + viscosity * (sx[c, part, :] + sy[c, part, :] + second)
        )
        return 0

    lax.fori_loop(0, nc * mx, solve_z, 0)

    for copy in second_round:
        copy.wait_recv()
    for c in range(nc):
        lines = my // 8
        outer = [
            [ti[way, pl.ds(s * per + c * lines, lines)].reshape(my, nz) for way in range(2)]
            for s in range(2)
        ]
        for i in range(mx):
            part = pl.ds(i * my, my)
            more = sys_x[0].low[i] * outer[0][0] + sys_x[0].high[i] * outer[0][1]
            bend = sys_x[1].low[i] * outer[1][0] + sys_x[1].high[i] * outer[1][1]
            moved = v[0, part, :] * more
            conv[c, part, :] = conv[c, part, :] + moved
            expl[c, part, :] = expl[c, part, :] + (viscosity * bend - (time_step * gamma_now) * moved)

    right_w = [pick(wall, sys_w.right[:, i]) for i in range(my)]
    left_w = [pick(wall, sys_w.left[:, i]) for i in range(my)]

    def sums_w(c, _):
        low = high = None
        for i in range(my):
            row = yrow(expl, c, i)
            low = right_w[i] * row if low is None else low + right_w[i] * row
            high = left_w[i] * row if high is None else high + left_w[i] * row
        gw[0, c] = low
        gw[1, c] = high
        return 0

    lax.fori_loop(0, nc, sums_w, 0)
    w_copies = []
    for d in range(1, py):
        copy = remote(gw, gwr.at[wall], ws.at[d], wr.at[d], gy=gy_peer(d))
        copy.start()
        w_copies.append(copy)
    gwr[wall] = gw[...]

    def solve_w(index, _):
        c = index // (mx // 8)
        base = lax.rem(index, mx // 8) * 8
        rows = [expl[c, pl.ds(base * my + y, 8, stride=my), :] for y in range(my)]
        for i, value in enumerate(sys_w.solve(rows)):
            upd[c, pl.ds(base * my + i, 8, stride=my), :] = value
        return 0

    lax.fori_loop(0, nc * (mx // 8), solve_w, 0)
    for copy in w_copies:
        copy.wait_recv()
    outer_w = [gathered(sys_w, side) for side in range(2)]

    def finish(c, _):
        ends = [
            total([
                outer_w[side][q][way] * gwr[q, way, c] for q in range(py) for way in range(2)
            ])
            for side in range(2)
        ]
        for i in range(my):
            at = pl.ds(i, mx, stride=my)
            upd[c, at, :] = upd[c, at, :] + (sys_w.low[i] * ends[0] + sys_w.high[i] * ends[1])
        return 0

    lax.fori_loop(0, nc, finish, 0)

    for copy, _ in first_round:
        copy.wait_send()
    for copy in second_round + z_copies + gy_copies + w_copies:
        copy.wait_send()

    @pl.when(me < px - 1)
    def _():
        up.wait_send()

    @pl.when(me > 0)
    def _():
        down.wait_send()

    @pl.when(wall < py - 1)
    def _():
        y_up.wait_send()

    @pl.when(wall > 0)
    def _():
        y_down.wait_send()


def body(counts, velocity, conv_prev):
    px, py, pz = counts
    nc, mx, my, nz = velocity.shape
    assert pz == 2 and my % 8 == 0 and mx % 8 == 0
    real = 2 * nc * (my // 8)
    units = -(-real // px)
    assert (real // 2) % units == 0
    flat = (nc, mx * my, nz)
    f32 = jnp.float32

    def vmem(*shape):
        return pltpu.VMEM(shape, f32)

    def dma(n):
        return pltpu.SemaphoreType.DMA((n,))

    whole = pl.BlockSpec(memory_space=pltpu.VMEM)
    conv, upd = pl.pallas_call(
        functools.partial(kernel, (nc, mx, my, nz, px, py, units)),
        out_shape=[jax.ShapeDtypeStruct(flat, f32)] * 2,
        in_specs=[whole, whole],
        out_specs=[whole, whole],
        scratch_shapes=[
            vmem(*flat),
            vmem(nc, 2 * my, nz), vmem(nc, 2 * my, nz),
            vmem(2, 2, nc, mx, nz), vmem(2, nc, mx, nz), vmem(2, nc, mx, nz),
            vmem(2, px * units, 8, nz), vmem(px, 2, units, 8, nz),
            vmem(px, 2, units, 8, nz), vmem(2, px * units, 8, nz),
            vmem(2, 2, nc, mx, nz), vmem(py, 2, 2, nc, mx, nz),
            vmem(2, nc, mx, nz), vmem(py, 2, nc, mx, nz),
            vmem(*flat), vmem(*flat), vmem(*flat), vmem(*flat), vmem(*flat),
            dma(px), dma(px), dma(px), dma(px), dma(2), dma(2), dma(2), dma(2),
            dma(py), dma(py), dma(py), dma(py), dma(nc), dma(nc),
        ],
        compiler_params=pltpu.CompilerParams(
            collective_id=0, has_side_effects=True, vmem_limit_bytes=32 * 1024 * 1024
        ),
    )(velocity.reshape(flat), conv_prev.reshape(flat))
    return conv.reshape(velocity.shape), upd.reshape(velocity.shape)


def solution(mesh):
    spec = P(None, "gx", "gy", "gz")
    counts = tuple(mesh.shape[name] for name in ("gx", "gy", "gz"))
    return jax.shard_map(
        functools.partial(body, counts), mesh=mesh, in_specs=(spec, spec),
        out_specs=(spec, spec), check_vma=False,
    )
```

```python
import collections
import functools

import jax
import jax.numpy as jnp
import numpy as np
from jax import lax
from jax.experimental import pallas as pl
from jax.experimental.pallas import tpu as pltpu
from jax.sharding import PartitionSpec as P

MESH = pl.DeviceIdType.MESH
WIDE = 8
time_step = 1.0
gamma_now = 5.0 / 12.0
zeta_old = -17.0 / 60.0
viscosity = 0.1

FIRST = {1: 7.0 / 9.0, -1: -7.0 / 9.0, 2: 1.0 / 36.0, -2: -1.0 / 36.0}
SECOND = {1: 12.0 / 11.0, -1: 12.0 / 11.0, 2: 3.0 / 44.0, -2: 3.0 / 44.0, 0: -24.0 / 11.0 - 6.0 / 44.0}
COMPACT = ((1.0 / 3.0, 1.0, FIRST), (2.0 / 11.0, 1.0, SECOND))


class System:
    def __init__(self, off, mid, stencil, count, m):
        n = count * m
        rho = np.zeros(n + 2)
        last = 0.0
        for j in range(n + 2):
            last = -off / (mid + off * last)
            rho[j] = last

        def u(j, ref):
            if j < 0:
                return 0.0
            if j <= ref:
                return float(np.prod(rho[j:ref]))
            return 1.0 / float(np.prod(rho[ref:j]))

        def v(j, ref):
            return u(n - 1 - j, n - 1 - ref)

        def inv(i, j):
            low = rho[i - 1] if i > 0 else 0.0
            high = rho[n - 2 - i] if i < n - 1 else 0.0
            diag = 1.0 / (mid + off * low + off * high)
            return diag * (u(j, i) if j <= i else v(j, i))

        def b(j, col):
            return stencil.get(col - j, 0.0)

        self.off, self.m, self.count = off, m, count
        self.right, self.left = np.zeros((count, m)), np.zeros((count, m))
        self.fix_low, self.fix_high = np.zeros((count, 3)), np.zeros((count, 3))
        self.d = np.zeros((count, 4))
        self.t = np.zeros((count, 2))
        self.weights = np.zeros((2, count, 2, count))
        for p in range(count):
            start, end = p * m, p * m + m - 1
            for k in range(m):
                col = start + k
                rows = [j for j in range(col - 2, col + 3) if 0 <= j < n]
                self.right[p, k] = sum(u(j, end) * b(j, col) for j in rows)
                self.left[p, k] = sum(v(j, start) * b(j, col) for j in rows)
            if p > 0:
                e = start - 1
                self.fix_low[p] = (
                    sum((inv(e, j) - inv(e, e) * u(j, e)) * b(j, e) for j in (e + 1, e + 2)),
                    (inv(e, e + 1) - inv(e, e) * u(e + 1, e)) * b(e + 1, e - 1),
                    (inv(e, e - 1) - inv(e, e + 1) * v(e - 1, e + 1)) * b(e - 1, e + 1),
                )
                self.d[p, 0], self.d[p, 1] = inv(e, e), inv(e, e + 1)
                self.t[p, 0] = u(e, end)
                for q in range(count):
                    if q < p:
                        self.weights[0, q, 0, p] = inv(e, q * m + m - 1)
                    else:
                        self.weights[0, q, 1, p] = inv(e, q * m)
            if p < count - 1:
                f = end + 1
                self.fix_high[p] = (
                    sum((inv(f, j) - inv(f, f) * v(j, f)) * b(j, f) for j in (f - 1, f - 2)),
                    (inv(f, f - 1) - inv(f, f) * v(f - 1, f)) * b(f - 1, f + 1),
                    (inv(f, f + 1) - inv(f, f - 1) * u(f + 1, f - 1)) * b(f + 1, f - 1),
                )
                self.d[p, 2], self.d[p, 3] = inv(f, f - 1), inv(f, f)
                self.t[p, 1] = v(f, start)
                for q in range(count):
                    if q > p:
                        self.weights[1, q, 1, p] = inv(f, q * m)
                    else:
                        self.weights[1, q, 0, p] = inv(f, q * m + m - 1)
        pivots, ratios, last = [], [], 0.0
        for _ in range(m):
            pivot = mid - off * last
            last = off / pivot
            pivots.append(pivot)
            ratios.append(last)
        self.scale = [float(1.0 / pivot) for pivot in pivots]
        self.ratio = [float(ratio) for ratio in ratios]
        unit = np.zeros(m)
        unit[0] = 1.0
        self.low = [-off * value for value in self.solve(list(unit))]
        self.high = self.low[::-1]

    def solve(self, rows):
        done, carry = [], None
        for i, row in enumerate(rows):
            fresh = row * self.scale[i]
            carry = fresh if carry is None else fresh - self.ratio[i] * carry
            done.append(carry)
        for i in range(self.m - 2, -1, -1):
            done[i] = done[i] - self.ratio[i] * done[i + 1]
        return done


def pick(place, values):
    values = [float(np.float32(value)) for value in values]
    common = collections.Counter(values).most_common(1)[0][0]
    result = jnp.float32(common)
    for index, value in enumerate(values):
        if value != common:
            result = jnp.where(place == index, jnp.float32(value), result)
    return result


def sides(at):
    odd_1, even_1 = at(1) - at(-1), at(1) + at(-1)
    odd_2, even_2 = at(2) - at(-2), at(2) + at(-2)
    first = FIRST[1] * odd_1 + FIRST[2] * odd_2
    second = SECOND[1] * even_1 + (SECOND[2] * even_2 + SECOND[0] * at(0))
    return first, second


def total(terms):
    return functools.reduce(lambda a, b: a + b, terms)


def kernel(
    cfg, v_hbm, cp_hbm, conv, upd,
    v, cp, load,
    wz, vt, zo, xlo, xhi, ylo, yhi, gx, gr, to, ti, gy, gyr, gw, gwr,
    fx, sx, fy, sy, expl, et,
    t1s, t1r, t2s, t2r, xs, xr, ys, yr, gys, gyrs, ws, wr, zs, zr,
):
    nc, mx, my, nz, px, py, units = cfg
    real = len(COMPACT) * nc * (my // 8)
    me = lax.axis_index("gx")
    wall = lax.axis_index("gy")
    core = lax.axis_index("gz")
    sys_x = [System(*pair, px, mx) for pair in COMPACT]
    sys_y = [System(*pair, py, my) for pair in COMPACT]
    beta = 4.0 * my * my
    sys_w = System(-beta, 1.0 + 2.0 * beta, {0: 1.0}, py, my)

    reads = [pltpu.make_async_copy(v_hbm.at[c], v.at[c], load.at[c]) for c in range(nc)]
    reads_cp = [pltpu.make_async_copy(cp_hbm.at[c], cp.at[c], load.at[nc + c]) for c in range(nc)]
    for read in reads + reads_cp:
        read.start()

    def gx_peer(d):
        return lax.rem(me + d, px)

    def gy_peer(d):
        return lax.rem(wall + d, py)

    barrier = pltpu.get_barrier_semaphore()
    for d in range(1, px):
        pl.semaphore_signal(barrier, inc=1, device_id={"gx": gx_peer(d)}, device_id_type=MESH)
    for d in range(1, py):
        pl.semaphore_signal(barrier, inc=1, device_id={"gy": gy_peer(d)}, device_id_type=MESH)
    pl.semaphore_signal(barrier, inc=1, device_id={"gz": 1 - core}, device_id_type=MESH)

    def remote(src, dst, send, recv, **target):
        return pltpu.make_async_remote_copy(
            src_ref=src, dst_ref=dst, send_sem=send, recv_sem=recv,
            device_id=target, device_id_type=MESH,
        )

    for read in reads:
        read.wait()

    per = nc * (my // 8)
    weigh_x = [
        [[pick(me, table[:, i]) for i in range(mx)] for table in (s.right, s.left)] for s in sys_x
    ]

    def sums_x(c, _):
        rows = [v[c, pl.ds(i * my, my), :] for i in range(mx)]
        for s in range(2):
            for way in range(2):
                value = total([weigh_x[s][way][i] * rows[i] for i in range(mx)])
                gx[way, pl.ds(s * per + c * (my // 8), my // 8)] = value.reshape(my // 8, 8, nz)
        return 0

    lax.fori_loop(0, nc, sums_x, 0)
    if px * units > real:
        gx[:, pl.ds(real, px * units - real)] = jnp.zeros((2, px * units - real, 8, nz), jnp.float32)

    size = (2 * nz, 2 * nz)
    source = lax.broadcasted_iota(jnp.int32, size, 0)
    target = lax.broadcasted_iota(jnp.int32, size, 1)
    is_first = target < nz
    gap = source - jnp.where(is_first, target, target - nz)
    gap = jnp.where((source >= nz) & (gap > nz), gap - 2 * nz, gap)
    far = jnp.abs(gap)
    odd = jnp.where(far == 1, 45.0, jnp.where(far == 2, -9.0, jnp.where(far == 3, 1.0, 0.0)))
    odd = jnp.where(gap < 0, -odd, odd)
    even = jnp.where(
        far == 0, -490.0,
        jnp.where(far == 1, 270.0, jnp.where(far == 2, -27.0, jnp.where(far == 3, 2.0, 0.0))),
    )
    wz[...] = jnp.where(is_first, odd, even).astype(jnp.bfloat16)

    pl.semaphore_wait(barrier, px - 1 + py - 1 + 1)

    first_round = []
    for d in range(1, px):
        t = gx_peer(d)
        source = gx_peer(px - d)
        copy = remote(
            gx.at[:, pl.ds(t * units, units)], gr.at[me], t1s.at[d], t1r.at[d], gx=t
        )
        copy.start()
        first_round.append((copy, source))
    gr[me] = gx[:, pl.ds(me * units, units)]

    up = remote(v.at[:, pl.ds((mx - 2) * my, 2 * my)], xlo, xs.at[0], xr.at[0], gx=gx_peer(1))
    down = remote(v.at[:, pl.ds(0, 2 * my)], xhi, xs.at[1], xr.at[1], gx=gx_peer(px - 1))

    @pl.when(me < px - 1)
    def _():
        up.start()

    @pl.when(me > 0)
    def _():
        down.start()

    z_copies = []
    for c in range(nc):
        copy = remote(v.at[c], zo.at[c], zs.at[c], zr.at[c], gz=1 - core)
        copy.start()
        z_copies.append(copy)

    def yrow(ref, c, y):
        return ref[c, pl.ds(y, mx, stride=my), :]

    weigh_y = [
        [[pick(wall, table[:, i]) for i in range(my)] for table in (s.right, s.left)] for s in sys_y
    ]

    def sums_y(c, _):
        sums = [[None, None], [None, None]]
        for i in range(my):
            row = yrow(v, c, i)
            vt[c, i] = row
            for s in range(2):
                for way in range(2):
                    term = weigh_y[s][way][i] * row
                    sums[s][way] = term if i == 0 else sums[s][way] + term
        for s in range(2):
            for way in range(2):
                gy[way, s, c] = sums[s][way]
        return 0

    lax.fori_loop(0, nc, sums_y, 0)
    y_up = remote(vt.at[:, pl.ds(my - 2, 2)], ylo, ys.at[0], yr.at[0], gy=gy_peer(1))
    y_down = remote(vt.at[:, pl.ds(0, 2)], yhi, ys.at[1], yr.at[1], gy=gy_peer(py - 1))

    @pl.when(wall < py - 1)
    def _():
        y_up.start()

    @pl.when(wall > 0)
    def _():
        y_down.start()

    gy_copies = []
    for d in range(1, py):
        copy = remote(gy, gyr.at[wall], gys.at[d], gyrs.at[d], gy=gy_peer(d))
        copy.start()
        gy_copies.append(copy)
    gyr[wall] = gy[...]

    @pl.when(wall > 0)
    def _():
        y_up.wait_recv()

    @pl.when(wall == 0)
    def _():
        ylo[...] = jnp.zeros_like(ylo)

    @pl.when(wall < py - 1)
    def _():
        y_down.wait_recv()

    @pl.when(wall == py - 1)
    def _():
        yhi[...] = jnp.zeros_like(yhi)

    for copy in gy_copies:
        copy.wait_recv()

    def gathered(system, side):
        return [[pick(wall, system.weights[side, q, way]) for way in range(2)] for q in range(py)]

    low_y = [[pick(wall, -s.off * s.fix_low[:, k]) for k in range(3)] for s in sys_y]
    high_y = [[pick(wall, -s.off * s.fix_high[:, k]) for k in range(3)] for s in sys_y]
    outer_y = [[gathered(s, side) for side in range(2)] for s in sys_y]

    wide = WIDE if mx % WIDE == 0 else 8

    def solve_y(index, _):
        c = index // (mx // wide)
        base = lax.rem(index, mx // wide) * wide
        part = pl.ds(base, wide)
        rows = [ylo[c, k, part, :] for k in range(2)]
        rows += [vt[c, y, part, :] for y in range(my)]
        rows += [yhi[c, k, part, :] for k in range(2)]
        pairs = [sides(lambda k, i=i: rows[i + 2 + k]) for i in range(my)]
        for s, out in ((0, fy), (1, sy)):
            rhs = [pair[s] for pair in pairs]
            ends = [
                total([
                    outer_y[s][side][q][way] * gyr[q, way, s, c, part, :]
                    for q in range(py) for way in range(2)
                ])
                for side in range(2)
            ]
            rhs[0] = rhs[0] + (
                low_y[s][0] * rows[1] + low_y[s][1] * rows[0] + low_y[s][2] * rows[2]
                - sys_y[s].off * ends[0]
            )
            rhs[my - 1] = rhs[my - 1] + (
                high_y[s][0] * rows[my + 2] + high_y[s][1] * rows[my + 3] + high_y[s][2] * rows[my + 1]
                - sys_y[s].off * ends[1]
            )
            for i, value in enumerate(sys_y[s].solve(rhs)):
                out[c, pl.ds(base * my + i, wide, stride=my), :] = value
        return 0

    lax.fori_loop(0, nc * (mx // wide), solve_y, 0)

    for copy, _ in first_round:
        copy.wait_recv()
    share = jnp.minimum(me * units // per, 1)

    def both(field):
        return [pick(share, [field(sys_x[0], p), field(sys_x[1], p)]) for p in range(px)]

    t0, t1 = (both(lambda s, p, k=k: s.t[p, k]) for k in range(2))
    d0, d1, d2, d3 = (both(lambda s, p, k=k: s.d[p, k]) for k in range(4))
    below, above = [None] * px, [None] * px
    for p in range(px):
        here = gr[p, 0]
        below[p] = here if p == 0 else here + t0[p] * below[p - 1]
    for p in reversed(range(px)):
        here = gr[p, 1]
        above[p] = here if p == px - 1 else here + t1[p] * above[p + 1]
    for p in range(px):
        zero = jnp.zeros((units, 8, nz), jnp.float32)
        to[p, 0] = zero if p == 0 else d0[p] * below[p - 1] + d1[p] * above[p]
        to[p, 1] = zero if p == px - 1 else d2[p] * below[p] + d3[p] * above[p + 1]
    second_round = []
    for d in range(1, px):
        t = gx_peer(d)
        copy = remote(to.at[t], ti.at[:, pl.ds(me * units, units)], t2s.at[d], t2r.at[d], gx=t)
        copy.start()
        second_round.append(copy)
    ti[:, pl.ds(me * units, units)] = to[me]

    @pl.when(me > 0)
    def _():
        up.wait_recv()

    @pl.when(me == 0)
    def _():
        xlo[...] = jnp.zeros_like(xlo)

    @pl.when(me < px - 1)
    def _():
        down.wait_recv()

    @pl.when(me == px - 1)
    def _():
        xhi[...] = jnp.zeros_like(xhi)

    low_x = [[pick(me, -s.off * s.fix_low[:, k]) for k in range(3)] for s in sys_x]
    high_x = [[pick(me, -s.off * s.fix_high[:, k]) for k in range(3)] for s in sys_x]
    tile = 16 if my % 16 == 0 else 8

    def solve_x(index, _):
        c = index // (my // tile)
        base = lax.rem(index, my // tile) * tile
        rows = [xlo[c, pl.ds(k * my + base, tile), :] for k in range(2)]
        rows += [v[c, pl.ds(i * my + base, tile), :] for i in range(mx)]
        rows += [xhi[c, pl.ds(k * my + base, tile), :] for k in range(2)]
        pairs = [sides(lambda k, i=i: rows[i + 2 + k]) for i in range(mx)]
        for s, out in ((0, fx), (1, sx)):
            rhs = [pair[s] for pair in pairs]
            rhs[0] = rhs[0] + (
                low_x[s][0] * rows[1] + low_x[s][1] * rows[0] + low_x[s][2] * rows[2]
            )
            rhs[mx - 1] = rhs[mx - 1] + (
                high_x[s][0] * rows[mx + 2] + high_x[s][1] * rows[mx + 3] + high_x[s][2] * rows[mx + 1]
            )
            for i, value in enumerate(sys_x[s].solve(rhs)):
                out[c, pl.ds(i * my + base, tile), :] = value
        return 0

    lax.fori_loop(0, nc * (my // tile), solve_x, 0)

    for copy in z_copies:
        copy.wait_recv()

    for read in reads_cp:
        read.wait()
    slab = 4 * my

    def solve_z(index, _):
        c = index // (mx * my // slab)
        part = pl.ds(lax.rem(index, mx * my // slab) * slab, slab)
        own = v[c, part, :]
        rest = jnp.concatenate([own, zo[c, part, :]], axis=1)
        both_z = None
        for step in range(3):
            piece = rest.astype(jnp.bfloat16)
            product = jnp.dot(piece, wz[...], preferred_element_type=jnp.float32)
            both_z = product if both_z is None else both_z + product
            if step < 2:
                rest = rest - piece.astype(jnp.float32)
        first = both_z[:, :nz] * (1.0 / 60.0)
        second = both_z[:, nz:] * (1.0 / 180.0)
        moved = v[0, part, :] * fx[c, part, :] + v[1, part, :] * fy[c, part, :] + v[2, part, :] * first
        conv[c, part, :] = moved
        expl[c, part, :] = (
            own - time_step * (gamma_now * moved + zeta_old * cp[c, part, :])
            + viscosity * (sx[c, part, :] + sy[c, part, :] + second)
        )
        return 0

    lax.fori_loop(0, nc * mx * my // slab, solve_z, 0)

    for copy in second_round:
        copy.wait_recv()
    for c in range(nc):
        lines = my // 8
        outer = [
            [ti[way, pl.ds(s * per + c * lines, lines)].reshape(my, nz) for way in range(2)]
            for s in range(2)
        ]
        for i in range(mx):
            part = pl.ds(i * my, my)
            more = sys_x[0].low[i] * outer[0][0] + sys_x[0].high[i] * outer[0][1]
            bend = sys_x[1].low[i] * outer[1][0] + sys_x[1].high[i] * outer[1][1]
            moved = v[0, part, :] * more
            conv[c, part, :] = conv[c, part, :] + moved
            expl[c, part, :] = expl[c, part, :] + (viscosity * bend - (time_step * gamma_now) * moved)

    right_w = [pick(wall, sys_w.right[:, i]) for i in range(my)]
    left_w = [pick(wall, sys_w.left[:, i]) for i in range(my)]

    def sums_w(c, _):
        low = high = None
        for i in range(my):
            row = yrow(expl, c, i)
            et[c, i] = row
            low = right_w[i] * row if low is None else low + right_w[i] * row
            high = left_w[i] * row if high is None else high + left_w[i] * row
        gw[0, c] = low
        gw[1, c] = high
        return 0

    lax.fori_loop(0, nc, sums_w, 0)
    w_copies = []
    for d in range(1, py):
        copy = remote(gw, gwr.at[wall], ws.at[d], wr.at[d], gy=gy_peer(d))
        copy.start()
        w_copies.append(copy)
    gwr[wall] = gw[...]

    def solve_w(index, _):
        rows = [et[index, y] for y in range(my)]
        for i, value in enumerate(sys_w.solve(rows)):
            et[index, i] = value
        return 0

    lax.fori_loop(0, nc, solve_w, 0)
    for copy in w_copies:
        copy.wait_recv()
    outer_w = [gathered(sys_w, side) for side in range(2)]

    def finish(c, _):
        ends = [
            total([
                outer_w[side][q][way] * gwr[q, way, c] for q in range(py) for way in range(2)
            ])
            for side in range(2)
        ]
        for i in range(my):
            at = pl.ds(i, mx, stride=my)
            upd[c, at, :] = et[c, i] + (sys_w.low[i] * ends[0] + sys_w.high[i] * ends[1])
        return 0

    lax.fori_loop(0, nc, finish, 0)

    for copy, _ in first_round:
        copy.wait_send()
    for copy in second_round + z_copies + gy_copies + w_copies:
        copy.wait_send()

    @pl.when(me < px - 1)
    def _():
        up.wait_send()

    @pl.when(me > 0)
    def _():
        down.wait_send()

    @pl.when(wall < py - 1)
    def _():
        y_up.wait_send()

    @pl.when(wall > 0)
    def _():
        y_down.wait_send()


def body(counts, velocity, conv_prev):
    px, py, pz = counts
    nc, mx, my, nz = velocity.shape
    assert pz == 2 and my % 8 == 0 and mx % 8 == 0
    real = 2 * nc * (my // 8)
    units = -(-real // px)
    assert (real // 2) % units == 0
    flat = (nc, mx * my, nz)
    f32 = jnp.float32

    def vmem(*shape):
        return pltpu.VMEM(shape, f32)

    def dma(n):
        return pltpu.SemaphoreType.DMA((n,))

    whole = pl.BlockSpec(memory_space=pltpu.VMEM)
    velocity = pltpu.with_memory_space_constraint(velocity.reshape(flat), pltpu.HBM)
    conv_prev = pltpu.with_memory_space_constraint(conv_prev.reshape(flat), pltpu.HBM)
    hbm = pl.BlockSpec(memory_space=pltpu.HBM)
    conv, upd = pl.pallas_call(
        functools.partial(kernel, (nc, mx, my, nz, px, py, units)),
        out_shape=[jax.ShapeDtypeStruct(flat, f32)] * 2,
        in_specs=[hbm, hbm],
        out_specs=[whole, whole],
        scratch_shapes=[
            vmem(*flat), vmem(*flat), dma(2 * nc),
            pltpu.VMEM((2 * nz, 2 * nz), jnp.bfloat16), vmem(nc, my, mx, nz), vmem(*flat),
            vmem(nc, 2 * my, nz), vmem(nc, 2 * my, nz),
            vmem(nc, 2, mx, nz), vmem(nc, 2, mx, nz),
            vmem(2, px * units, 8, nz), vmem(px, 2, units, 8, nz),
            vmem(px, 2, units, 8, nz), vmem(2, px * units, 8, nz),
            vmem(2, 2, nc, mx, nz), vmem(py, 2, 2, nc, mx, nz),
            vmem(2, nc, mx, nz), vmem(py, 2, nc, mx, nz),
            vmem(*flat), vmem(*flat), vmem(*flat), vmem(*flat), vmem(*flat), vmem(nc, my, mx, nz),
            dma(px), dma(px), dma(px), dma(px), dma(2), dma(2), dma(2), dma(2),
            dma(py), dma(py), dma(py), dma(py), dma(nc), dma(nc),
        ],
        compiler_params=pltpu.CompilerParams(
            collective_id=0, has_side_effects=True, vmem_limit_bytes=32 * 1024 * 1024
        ),
    )(velocity, conv_prev)
    return conv.reshape(nc, mx, my, nz), upd.reshape(nc, mx, my, nz)


def solution(mesh):
    spec = P(None, "gx", "gy", "gz")
    counts = tuple(mesh.shape[name] for name in ("gx", "gy", "gz"))
    return jax.shard_map(
        functools.partial(body, counts), mesh=mesh, in_specs=(spec, spec),
        out_specs=(spec, spec), check_vma=False,
    )
```

```python
import collections
import functools

import jax
import jax.numpy as jnp
import numpy as np
from jax import lax
from jax.experimental import pallas as pl
from jax.experimental.pallas import tpu as pltpu
from jax.sharding import PartitionSpec as P

MESH = pl.DeviceIdType.MESH
WIDE = 8
time_step = 1.0
gamma_now = 5.0 / 12.0
zeta_old = -17.0 / 60.0
viscosity = 0.1

FIRST = {1: 7.0 / 9.0, -1: -7.0 / 9.0, 2: 1.0 / 36.0, -2: -1.0 / 36.0}
SECOND = {1: 12.0 / 11.0, -1: 12.0 / 11.0, 2: 3.0 / 44.0, -2: 3.0 / 44.0, 0: -24.0 / 11.0 - 6.0 / 44.0}
COMPACT = ((1.0 / 3.0, 1.0, FIRST), (2.0 / 11.0, 1.0, SECOND))


class System:
    def __init__(self, off, mid, stencil, count, m):
        n = count * m
        rho = np.zeros(n + 2)
        last = 0.0
        for j in range(n + 2):
            last = -off / (mid + off * last)
            rho[j] = last

        def u(j, ref):
            if j < 0:
                return 0.0
            if j <= ref:
                return float(np.prod(rho[j:ref]))
            return 1.0 / float(np.prod(rho[ref:j]))

        def v(j, ref):
            return u(n - 1 - j, n - 1 - ref)

        def inv(i, j):
            low = rho[i - 1] if i > 0 else 0.0
            high = rho[n - 2 - i] if i < n - 1 else 0.0
            diag = 1.0 / (mid + off * low + off * high)
            return diag * (u(j, i) if j <= i else v(j, i))

        def b(j, col):
            return stencil.get(col - j, 0.0)

        self.off, self.m, self.count = off, m, count
        self.right, self.left = np.zeros((count, m)), np.zeros((count, m))
        self.fix_low, self.fix_high = np.zeros((count, 3)), np.zeros((count, 3))
        self.d = np.zeros((count, 4))
        self.t = np.zeros((count, 2))
        self.weights = np.zeros((2, count, 2, count))
        for p in range(count):
            start, end = p * m, p * m + m - 1
            for k in range(m):
                col = start + k
                rows = [j for j in range(col - 2, col + 3) if 0 <= j < n]
                self.right[p, k] = sum(u(j, end) * b(j, col) for j in rows)
                self.left[p, k] = sum(v(j, start) * b(j, col) for j in rows)
            if p > 0:
                e = start - 1
                self.fix_low[p] = (
                    sum((inv(e, j) - inv(e, e) * u(j, e)) * b(j, e) for j in (e + 1, e + 2)),
                    (inv(e, e + 1) - inv(e, e) * u(e + 1, e)) * b(e + 1, e - 1),
                    (inv(e, e - 1) - inv(e, e + 1) * v(e - 1, e + 1)) * b(e - 1, e + 1),
                )
                self.d[p, 0], self.d[p, 1] = inv(e, e), inv(e, e + 1)
                self.t[p, 0] = u(e, end)
                for q in range(count):
                    if q < p:
                        self.weights[0, q, 0, p] = inv(e, q * m + m - 1)
                    else:
                        self.weights[0, q, 1, p] = inv(e, q * m)
            if p < count - 1:
                f = end + 1
                self.fix_high[p] = (
                    sum((inv(f, j) - inv(f, f) * v(j, f)) * b(j, f) for j in (f - 1, f - 2)),
                    (inv(f, f - 1) - inv(f, f) * v(f - 1, f)) * b(f - 1, f + 1),
                    (inv(f, f + 1) - inv(f, f - 1) * u(f + 1, f - 1)) * b(f + 1, f - 1),
                )
                self.d[p, 2], self.d[p, 3] = inv(f, f - 1), inv(f, f)
                self.t[p, 1] = v(f, start)
                for q in range(count):
                    if q > p:
                        self.weights[1, q, 1, p] = inv(f, q * m)
                    else:
                        self.weights[1, q, 0, p] = inv(f, q * m + m - 1)
        pivots, ratios, last = [], [], 0.0
        for _ in range(m):
            pivot = mid - off * last
            last = off / pivot
            pivots.append(pivot)
            ratios.append(last)
        self.scale = [float(1.0 / pivot) for pivot in pivots]
        self.ratio = [float(ratio) for ratio in ratios]
        unit = np.zeros(m)
        unit[0] = 1.0
        self.low = [-off * value for value in self.solve(list(unit))]
        self.high = self.low[::-1]

    def solve(self, rows):
        done, carry = [], None
        for i, row in enumerate(rows):
            fresh = row * self.scale[i]
            carry = fresh if carry is None else fresh - self.ratio[i] * carry
            done.append(carry)
        for i in range(self.m - 2, -1, -1):
            done[i] = done[i] - self.ratio[i] * done[i + 1]
        return done


def pick(place, values):
    values = [float(np.float32(value)) for value in values]
    common = collections.Counter(values).most_common(1)[0][0]
    result = jnp.float32(common)
    for index, value in enumerate(values):
        if value != common:
            result = jnp.where(place == index, jnp.float32(value), result)
    return result


def sides(at):
    odd_1, even_1 = at(1) - at(-1), at(1) + at(-1)
    odd_2, even_2 = at(2) - at(-2), at(2) + at(-2)
    first = FIRST[1] * odd_1 + FIRST[2] * odd_2
    second = SECOND[1] * even_1 + (SECOND[2] * even_2 + SECOND[0] * at(0))
    return first, second


def total(terms):
    return functools.reduce(lambda a, b: a + b, terms)


def kernel(
    cfg, v_hbm, cp_hbm, conv, upd,
    v, cp, load,
    wz, vt, zo, xlo, xhi, ylo, yhi, gx, gr, to, ti, gy, gyr, gw, gwr,
    fx, sx, fy, sy, expl, et,
    t1s, t1r, t2s, t2r, xs, xr, ys, yr, gys, gyrs, ws, wr, zs, zr,
):
    nc, mx, my, nz, px, py, units = cfg
    real = len(COMPACT) * nc * (my // 8)
    me = lax.axis_index("gx")
    wall = lax.axis_index("gy")
    core = lax.axis_index("gz")
    sys_x = [System(*pair, px, mx) for pair in COMPACT]
    sys_y = [System(*pair, py, my) for pair in COMPACT]
    beta = 4.0 * my * my
    sys_w = System(-beta, 1.0 + 2.0 * beta, {0: 1.0}, py, my)

    reads = [pltpu.make_async_copy(v_hbm.at[c], v.at[c], load.at[c]) for c in range(nc)]
    reads_cp = [pltpu.make_async_copy(cp_hbm.at[c], cp.at[c], load.at[nc + c]) for c in range(nc)]
    for read in reads + reads_cp:
        read.start()

    def gx_peer(d):
        return lax.rem(me + d, px)

    def gy_peer(d):
        return lax.rem(wall + d, py)

    barrier = pltpu.get_barrier_semaphore()
    for d in range(1, px):
        pl.semaphore_signal(barrier, inc=1, device_id={"gx": gx_peer(d)}, device_id_type=MESH)
    for d in range(1, py):
        pl.semaphore_signal(barrier, inc=1, device_id={"gy": gy_peer(d)}, device_id_type=MESH)
    pl.semaphore_signal(barrier, inc=1, device_id={"gz": 1 - core}, device_id_type=MESH)

    def remote(src, dst, send, recv, **target):
        return pltpu.make_async_remote_copy(
            src_ref=src, dst_ref=dst, send_sem=send, recv_sem=recv,
            device_id=target, device_id_type=MESH,
        )

    for read in reads:
        read.wait()

    per = nc * (my // 8)
    weigh_x = [
        [[pick(me, table[:, i]) for i in range(mx)] for table in (s.right, s.left)] for s in sys_x
    ]

    def sums_x(c, _):
        rows = [v[c, pl.ds(i * my, my), :] for i in range(mx)]
        for s in range(2):
            for way in range(2):
                value = total([weigh_x[s][way][i] * rows[i] for i in range(mx)])
                gx[way, pl.ds(s * per + c * (my // 8), my // 8)] = value.reshape(my // 8, 8, nz)
        return 0

    lax.fori_loop(0, nc, sums_x, 0)
    if px * units > real:
        gx[:, pl.ds(real, px * units - real)] = jnp.zeros((2, px * units - real, 8, nz), jnp.float32)

    size = (2 * nz, 2 * nz)
    source = lax.broadcasted_iota(jnp.int32, size, 0)
    target = lax.broadcasted_iota(jnp.int32, size, 1)
    is_first = target < nz
    gap = source - jnp.where(is_first, target, target - nz)
    gap = jnp.where((source >= nz) & (gap > nz), gap - 2 * nz, gap)
    far = jnp.abs(gap)
    odd = jnp.where(far == 1, 45.0, jnp.where(far == 2, -9.0, jnp.where(far == 3, 1.0, 0.0)))
    odd = jnp.where(gap < 0, -odd, odd)
    even = jnp.where(
        far == 0, -490.0,
        jnp.where(far == 1, 270.0, jnp.where(far == 2, -27.0, jnp.where(far == 3, 2.0, 0.0))),
    )
    wz[...] = jnp.where(is_first, odd, even).astype(jnp.bfloat16)

    pl.semaphore_wait(barrier, px - 1 + py - 1 + 1)

    first_round = []
    for d in range(1, px):
        t = gx_peer(d)
        source = gx_peer(px - d)
        copy = remote(
            gx.at[:, pl.ds(t * units, units)], gr.at[me], t1s.at[d], t1r.at[d], gx=t
        )
        copy.start()
        first_round.append((copy, source))
    gr[me] = gx[:, pl.ds(me * units, units)]

    up = remote(v.at[:, pl.ds((mx - 2) * my, 2 * my)], xlo, xs.at[0], xr.at[0], gx=gx_peer(1))
    down = remote(v.at[:, pl.ds(0, 2 * my)], xhi, xs.at[1], xr.at[1], gx=gx_peer(px - 1))

    @pl.when(me < px - 1)
    def _():
        up.start()

    @pl.when(me > 0)
    def _():
        down.start()

    z_copies = []
    for c in range(nc):
        copy = remote(v.at[c], zo.at[c], zs.at[c], zr.at[c], gz=1 - core)
        copy.start()
        z_copies.append(copy)

    def yrow(ref, c, y):
        return ref[c, pl.ds(y, mx, stride=my), :]

    weigh_y = [
        [[pick(wall, table[:, i]) for i in range(my)] for table in (s.right, s.left)] for s in sys_y
    ]

    def sums_y(c, _):
        sums = [[None, None], [None, None]]
        for i in range(my):
            row = yrow(v, c, i)
            vt[c, i] = row
            for s in range(2):
                for way in range(2):
                    term = weigh_y[s][way][i] * row
                    sums[s][way] = term if i == 0 else sums[s][way] + term
        for s in range(2):
            for way in range(2):
                gy[way, s, c] = sums[s][way]
        return 0

    lax.fori_loop(0, nc, sums_y, 0)
    y_up = remote(vt.at[:, pl.ds(my - 2, 2)], ylo, ys.at[0], yr.at[0], gy=gy_peer(1))
    y_down = remote(vt.at[:, pl.ds(0, 2)], yhi, ys.at[1], yr.at[1], gy=gy_peer(py - 1))

    @pl.when(wall < py - 1)
    def _():
        y_up.start()

    @pl.when(wall > 0)
    def _():
        y_down.start()

    gy_copies = []
    for d in range(1, py):
        copy = remote(gy, gyr.at[wall], gys.at[d], gyrs.at[d], gy=gy_peer(d))
        copy.start()
        gy_copies.append(copy)
    gyr[wall] = gy[...]

    @pl.when(wall > 0)
    def _():
        y_up.wait_recv()

    @pl.when(wall == 0)
    def _():
        ylo[...] = jnp.zeros_like(ylo)

    @pl.when(wall < py - 1)
    def _():
        y_down.wait_recv()

    @pl.when(wall == py - 1)
    def _():
        yhi[...] = jnp.zeros_like(yhi)

    for copy in gy_copies:
        copy.wait_recv()

    def gathered(system, side):
        return [[pick(wall, system.weights[side, q, way]) for way in range(2)] for q in range(py)]

    low_y = [[pick(wall, -s.off * s.fix_low[:, k]) for k in range(3)] for s in sys_y]
    high_y = [[pick(wall, -s.off * s.fix_high[:, k]) for k in range(3)] for s in sys_y]
    outer_y = [[gathered(s, side) for side in range(2)] for s in sys_y]

    wide = WIDE if mx % WIDE == 0 else 8

    def solve_y(index, _):
        c = index // (mx // wide)
        base = lax.rem(index, mx // wide) * wide
        part = pl.ds(base, wide)
        rows = [ylo[c, k, part, :] for k in range(2)]
        rows += [vt[c, y, part, :] for y in range(my)]
        rows += [yhi[c, k, part, :] for k in range(2)]
        pairs = [sides(lambda k, i=i: rows[i + 2 + k]) for i in range(my)]
        for s, out in ((0, fy), (1, sy)):
            rhs = [pair[s] for pair in pairs]
            ends = [
                total([
                    outer_y[s][side][q][way] * gyr[q, way, s, c, part, :]
                    for q in range(py) for way in range(2)
                ])
                for side in range(2)
            ]
            rhs[0] = rhs[0] + (
                low_y[s][0] * rows[1] + low_y[s][1] * rows[0] + low_y[s][2] * rows[2]
                - sys_y[s].off * ends[0]
            )
            rhs[my - 1] = rhs[my - 1] + (
                high_y[s][0] * rows[my + 2] + high_y[s][1] * rows[my + 3] + high_y[s][2] * rows[my + 1]
                - sys_y[s].off * ends[1]
            )
            for i, value in enumerate(sys_y[s].solve(rhs)):
                out[c, pl.ds(base * my + i, wide, stride=my), :] = value
        return 0

    lax.fori_loop(0, nc * (mx // wide), solve_y, 0)

    for copy, _ in first_round:
        copy.wait_recv()
    share = jnp.minimum(me * units // per, 1)

    def both(field):
        return [pick(share, [field(sys_x[0], p), field(sys_x[1], p)]) for p in range(px)]

    t0, t1 = (both(lambda s, p, k=k: s.t[p, k]) for k in range(2))
    d0, d1, d2, d3 = (both(lambda s, p, k=k: s.d[p, k]) for k in range(4))
    below, above = [None] * px, [None] * px
    for p in range(px):
        here = gr[p, 0]
        below[p] = here if p == 0 else here + t0[p] * below[p - 1]
    for p in reversed(range(px)):
        here = gr[p, 1]
        above[p] = here if p == px - 1 else here + t1[p] * above[p + 1]
    for p in range(px):
        zero = jnp.zeros((units, 8, nz), jnp.float32)
        to[p, 0] = zero if p == 0 else d0[p] * below[p - 1] + d1[p] * above[p]
        to[p, 1] = zero if p == px - 1 else d2[p] * below[p] + d3[p] * above[p + 1]
    second_round = []
    for d in range(1, px):
        t = gx_peer(d)
        copy = remote(to.at[t], ti.at[:, pl.ds(me * units, units)], t2s.at[d], t2r.at[d], gx=t)
        copy.start()
        second_round.append(copy)
    ti[:, pl.ds(me * units, units)] = to[me]

    @pl.when(me > 0)
    def _():
        up.wait_recv()

    @pl.when(me == 0)
    def _():
        xlo[...] = jnp.zeros_like(xlo)

    @pl.when(me < px - 1)
    def _():
        down.wait_recv()

    @pl.when(me == px - 1)
    def _():
        xhi[...] = jnp.zeros_like(xhi)

    low_x = [[pick(me, -s.off * s.fix_low[:, k]) for k in range(3)] for s in sys_x]
    high_x = [[pick(me, -s.off * s.fix_high[:, k]) for k in range(3)] for s in sys_x]
    tile = 16 if my % 16 == 0 else 8

    def solve_x(index, _):
        c = index // (my // tile)
        base = lax.rem(index, my // tile) * tile
        rows = [xlo[c, pl.ds(k * my + base, tile), :] for k in range(2)]
        rows += [v[c, pl.ds(i * my + base, tile), :] for i in range(mx)]
        rows += [xhi[c, pl.ds(k * my + base, tile), :] for k in range(2)]
        pairs = [sides(lambda k, i=i: rows[i + 2 + k]) for i in range(mx)]
        for s, out in ((0, fx), (1, sx)):
            rhs = [pair[s] for pair in pairs]
            rhs[0] = rhs[0] + (
                low_x[s][0] * rows[1] + low_x[s][1] * rows[0] + low_x[s][2] * rows[2]
            )
            rhs[mx - 1] = rhs[mx - 1] + (
                high_x[s][0] * rows[mx + 2] + high_x[s][1] * rows[mx + 3] + high_x[s][2] * rows[mx + 1]
            )
            for i, value in enumerate(sys_x[s].solve(rhs)):
                out[c, pl.ds(i * my + base, tile), :] = value
        return 0

    lax.fori_loop(0, nc * (my // tile), solve_x, 0)

    for copy in z_copies:
        copy.wait_recv()

    for read in reads_cp:
        read.wait()
    slab = mx * my

    def solve_z(index, _):
        c = index // (mx * my // slab)
        part = pl.ds(lax.rem(index, mx * my // slab) * slab, slab)
        own = v[c, part, :]
        rest = jnp.concatenate([own, zo[c, part, :]], axis=1)
        pieces = []
        for step in range(3):
            pieces.append(rest.astype(jnp.bfloat16))
            if step < 2:
                rest = rest - pieces[-1].astype(jnp.float32)
        product = jnp.dot(
            jnp.concatenate(pieces, axis=0), wz[...], preferred_element_type=jnp.float32
        )
        both_z = product[:slab] + (product[slab : 2 * slab] + product[2 * slab :])
        first = both_z[:, :nz] * (1.0 / 60.0)
        second = both_z[:, nz:] * (1.0 / 180.0)
        moved = v[0, part, :] * fx[c, part, :] + v[1, part, :] * fy[c, part, :] + v[2, part, :] * first
        conv[c, part, :] = moved
        expl[c, part, :] = (
            own - time_step * (gamma_now * moved + zeta_old * cp[c, part, :])
            + viscosity * (sx[c, part, :] + sy[c, part, :] + second)
        )
        return 0

    lax.fori_loop(0, nc * mx * my // slab, solve_z, 0)

    right_w = [pick(wall, sys_w.right[:, i]) for i in range(my)]
    left_w = [pick(wall, sys_w.left[:, i]) for i in range(my)]

    w_copies = []
    for copy in second_round:
        copy.wait_recv()
    for c in range(nc):
        lines = my // 8
        outer = [
            [ti[way, pl.ds(s * per + c * lines, lines)].reshape(my, nz) for way in range(2)]
            for s in range(2)
        ]
        for i in range(mx):
            part = pl.ds(i * my, my)
            more = sys_x[0].low[i] * outer[0][0] + sys_x[0].high[i] * outer[0][1]
            bend = sys_x[1].low[i] * outer[1][0] + sys_x[1].high[i] * outer[1][1]
            moved = v[0, part, :] * more
            conv[c, part, :] = conv[c, part, :] + moved
            expl[c, part, :] = expl[c, part, :] + (viscosity * bend - (time_step * gamma_now) * moved)

        low = high = None
        for i in range(my):
            row = yrow(expl, c, i)
            et[c, i] = row
            low = right_w[i] * row if low is None else low + right_w[i] * row
            high = left_w[i] * row if high is None else high + left_w[i] * row
        gw[c, 0] = low
        gw[c, 1] = high
        copies = []
        for d in range(1, py):
            slot = (d - 1) * nc + c
            copy = remote(gw.at[c], gwr.at[wall, c], ws.at[slot], wr.at[slot], gy=gy_peer(d))
            copy.start()
            copies.append(copy)
        w_copies.append(copies)
        gwr[wall, c] = gw[c]

    def solve_w(index, _):
        rows = [et[index, y] for y in range(my)]
        for i, value in enumerate(sys_w.solve(rows)):
            et[index, i] = value
        return 0

    lax.fori_loop(0, nc, solve_w, 0)
    outer_w = [gathered(sys_w, side) for side in range(2)]

    for c in range(nc):
        for copy in w_copies[c]:
            copy.wait_recv()
        ends = [
            total([
                outer_w[side][q][way] * gwr[q, c, way] for q in range(py) for way in range(2)
            ])
            for side in range(2)
        ]
        for i in range(my):
            at = pl.ds(i, mx, stride=my)
            upd[c, at, :] = et[c, i] + (sys_w.low[i] * ends[0] + sys_w.high[i] * ends[1])

    for copy, _ in first_round:
        copy.wait_send()
    for copy in second_round + z_copies + gy_copies + sum(w_copies, []):
        copy.wait_send()

    @pl.when(me < px - 1)
    def _():
        up.wait_send()

    @pl.when(me > 0)
    def _():
        down.wait_send()

    @pl.when(wall < py - 1)
    def _():
        y_up.wait_send()

    @pl.when(wall > 0)
    def _():
        y_down.wait_send()


def body(counts, velocity, conv_prev):
    px, py, pz = counts
    nc, mx, my, nz = velocity.shape
    assert pz == 2 and my % 8 == 0 and mx % 8 == 0
    real = 2 * nc * (my // 8)
    units = -(-real // px)
    assert (real // 2) % units == 0
    flat = (nc, mx * my, nz)
    f32 = jnp.float32

    def vmem(*shape):
        return pltpu.VMEM(shape, f32)

    def dma(n):
        return pltpu.SemaphoreType.DMA((n,))

    whole = pl.BlockSpec(memory_space=pltpu.VMEM)
    velocity = pltpu.with_memory_space_constraint(velocity.reshape(flat), pltpu.HBM)
    conv_prev = pltpu.with_memory_space_constraint(conv_prev.reshape(flat), pltpu.HBM)
    hbm = pl.BlockSpec(memory_space=pltpu.HBM)
    conv, upd = pl.pallas_call(
        functools.partial(kernel, (nc, mx, my, nz, px, py, units)),
        out_shape=[jax.ShapeDtypeStruct(flat, f32)] * 2,
        in_specs=[hbm, hbm],
        out_specs=[whole, whole],
        scratch_shapes=[
            vmem(*flat), vmem(*flat), dma(2 * nc),
            pltpu.VMEM((2 * nz, 2 * nz), jnp.bfloat16), vmem(nc, my, mx, nz), vmem(*flat),
            vmem(nc, 2 * my, nz), vmem(nc, 2 * my, nz),
            vmem(nc, 2, mx, nz), vmem(nc, 2, mx, nz),
            vmem(2, px * units, 8, nz), vmem(px, 2, units, 8, nz),
            vmem(px, 2, units, 8, nz), vmem(2, px * units, 8, nz),
            vmem(2, 2, nc, mx, nz), vmem(py, 2, 2, nc, mx, nz),
            vmem(nc, 2, mx, nz), vmem(py, nc, 2, mx, nz),
            vmem(*flat), vmem(*flat), vmem(*flat), vmem(*flat), vmem(*flat), vmem(nc, my, mx, nz),
            dma(px), dma(px), dma(px), dma(px), dma(2), dma(2), dma(2), dma(2),
            dma(py), dma(py), dma(py * nc), dma(py * nc), dma(nc), dma(nc),
        ],
        compiler_params=pltpu.CompilerParams(
            collective_id=0, has_side_effects=True, vmem_limit_bytes=32 * 1024 * 1024
        ),
    )(velocity, conv_prev)
    return conv.reshape(nc, mx, my, nz), upd.reshape(nc, mx, my, nz)


def solution(mesh):
    spec = P(None, "gx", "gy", "gz")
    counts = tuple(mesh.shape[name] for name in ("gx", "gy", "gz"))
    return jax.shard_map(
        functools.partial(body, counts), mesh=mesh, in_specs=(spec, spec),
        out_specs=(spec, spec), check_vma=False,
    )
```
